32 devices in a mesh: ctx: 8 (over z, x), head: 4 (over y, core).
Axes of the slice: x: 2, y: 2, z: 4, core: 2. Of those that a mesh axis runs over, the one named last changes fastest.
Arguments:
- queries: bfloat16 [32768, 2048], P('ctx', 'head'), may hold values from -6 to 6
- keys: bfloat16 [32768, 2048], P('ctx', 'head'), may hold values from -6 to 6
- values: bfloat16 [32768, 2048], P('ctx', 'head'), may hold values from -6 to 6
- lam_index: int32 [512], P('ctx'), may hold values from 0 to 15
- level_weights: float32 [16, 16, 12], P(None, 'head'), may hold values from 0.25 to 2
- gate: bfloat16 [32768, 2048], P(('ctx', 'head')), may hold values from -6 to 6
- norm_gain: float32 [2048], replicated, may hold values from 0.25 to 1.75
- out_weight: bfloat16 [2048, 2048], P(None, ('ctx', 'head')), may hold values from -0.125 to 0.125
Outputs:
- output: bfloat16 [32768, 2048], P(('ctx', 'head'))
The draws below stay inside these ranges and needn't reach their ends.
All inputs are finite; a program needn't handle non-finite values.
Results may differ from the reference program's by a relative error of at most 0.0064.
Values may be sent and summed in bfloat16 or wider, within the bound.
No kernel may reach another device: no remote copies, remote signals or barrier semaphores. Data moves between devices by JAX's collectives and lax.ppermute only.
A program may use at most 192 MiB of HBM per device.

```python
import math
import jax
import jax.numpy as jnp
from jax import lax

HEADS = 16
DK = 128
D = 2048
SPAN = 64
LEVELS = 12
TABLE = 16
TOKENS = 32768
SPANS = 512


def touch_ends(drawn, stream_key, least, top_value):
    dims = drawn.shape
    index_at = [jax.random.randint(jax.random.fold_in(stream_key, axis), (), 0, dims[axis]) for axis in range(len(dims))]
    drawn = drawn.at[tuple(index_at)].set(least)
    longest = dims.index(max(dims))
    index_at[longest] = (index_at[longest] + 1) % dims[longest]
    return drawn.at[tuple(index_at)].set(top_value)


def steps_of(key, shape, shards, smallest, high):
    level, own = 1.0, jax.random.fold_in(key, 6)
    for dim, parts in shards:
        heights = jnp.exp(jax.random.uniform(jax.random.fold_in(own, dim), (parts,), jnp.float32, smallest / len(shards), high / len(shards)))
        level = level * jnp.repeat(heights, shape[dim] // parts).reshape([-1 if axis == dim else 1 for axis in range(len(shape))])
    return level


def noise(rng, dims, scale, reach, split=(), kind=jnp.bfloat16):
    result = jax.random.normal(rng, dims, jnp.float32) * scale
    if len(split) > 0:
        result = steps_of(rng, dims, split, -0.22, 0.18) * result
    return jnp.clip(result, min=-reach, max=reach).astype(kind)


def setup_inputs(seed: int = 0) -> dict:
    key_of = jax.random.split(jax.random.key(seed), 9)
    queries = noise(key_of[0], (TOKENS, D), 1.0, 6.0, ((0, 8), (1, 4)))
    keys = noise(key_of[1], (TOKENS, D), 1.0, 6.0, ((0, 8), (1, 4)))
    values = noise(key_of[2], (TOKENS, D), 1.0, 6.0, ((0, 8), (1, 4)))
    lam_index = touch_ends(jax.random.randint(key_of[3], (SPANS,), 0, TABLE), jax.random.fold_in(key_of[3], 1), 0, TABLE - 1).astype(jnp.int32)
    level_weights = jnp.clip(jnp.exp(math.log(2.0) - 2.0794415 * jax.random.uniform(key_of[4], (TABLE, HEADS, LEVELS), jnp.float32) ** steps_of(key_of[4], (TABLE, HEADS, LEVELS), ((1, 4),), -0.2, 0.2)), 0.25, 2.0)
    gate = noise(key_of[5], (TOKENS, D), 1.0, 6.0, ((0, 32),))
    norm_gain = jnp.clip(1.0 + 0.15 * jax.random.normal(key_of[6], (D,), jnp.float32), 0.25, 1.75)
    out_weight = noise(key_of[7], (D, D), D ** -0.5, 0.125, ((1, 32),))
    return dict(queries=queries, keys=keys, values=values, lam_index=lam_index, level_weights=level_weights, gate=gate, norm_gain=norm_gain, out_weight=out_weight)


def tree_mix(span_states, coefficient):
    total_count = span_states.shape[0]
    tail_shape = span_states.shape[1:]
    mixed = jnp.zeros_like(span_states)
    partial_value = span_states
    tree_level = 1
    block_width = 1
    while block_width < total_count:
        pair_count = total_count // (2 * block_width)
        paired = partial_value.reshape((pair_count, 2) + tail_shape)
        weight = coefficient[..., tree_level].reshape((pair_count, 2, block_width) + tail_shape[:-2])[:, 1]
        addend = weight[..., None, None] * paired[:, 0][:, None]
        mixed = mixed.reshape((pair_count, 2, block_width) + tail_shape).at[:, 1].add(addend)
        mixed = mixed.reshape((total_count,) + tail_shape)
        partial_value = paired[:, 0] + paired[:, 1]
        tree_level += 1
        block_width *= 2
    return (mixed, partial_value[0])

def reference(queries, keys, values, lam_index, level_weights, gate, norm_gain, out_weight):
    span_total = TOKENS // SPAN
    level_scale = jnp.exp2(-0.5 * jnp.arange(LEVELS, dtype=jnp.float32)) * DK ** (-0.5)
    coefficient = level_weights[lam_index] * level_scale
    causal = jnp.arange(SPAN)[:, None] >= jnp.arange(SPAN)[None, :]

    def per_head(head_id):
        query_blocks = lax.dynamic_slice_in_dim(queries, head_id * DK, DK, 1).reshape(span_total, SPAN, DK).astype(jnp.float32)
        key_blocks = lax.dynamic_slice_in_dim(keys, head_id * DK, DK, 1).reshape(span_total, SPAN, DK).astype(jnp.float32)
        value_blocks = lax.dynamic_slice_in_dim(values, head_id * DK, DK, 1).reshape(span_total, SPAN, DK).astype(jnp.float32)
        head_coef = coefficient[:, head_id, :]
        span_states = jnp.einsum('ctk,ctv->ckv', key_blocks, value_blocks)
        tree_state, unused_total = tree_mix(span_states, head_coef)
        rounded = lax.optimization_barrier(tree_state.astype(jnp.bfloat16)).astype(jnp.float32)
        carried = jnp.einsum('ctk,ckv->ctv', query_blocks, rounded)
        scores = jnp.einsum('csk,ctk->cst', query_blocks, key_blocks) * head_coef[:, 0][:, None, None]
        local_weights = jnp.where(causal[None], scores, 0.0).astype(jnp.bfloat16)
        local_weights = lax.optimization_barrier(local_weights).astype(jnp.float32)
        local_part = jnp.einsum('cst,ctv->csv', local_weights, value_blocks)
        return (local_part + carried).astype(jnp.bfloat16).reshape(TOKENS, DK)
    head_outputs = lax.map(per_head, jnp.arange(HEADS, dtype=jnp.int32))
    attention = head_outputs.transpose(1, 0, 2).reshape(TOKENS, D)
    gated = attention.astype(jnp.float32) * jax.nn.silu(gate.astype(jnp.float32))
    mean_square = lax.optimization_barrier(jnp.mean(gated * gated, axis=-1, keepdims=True))
    normed = (gated * lax.rsqrt(mean_square + 1e-06) * norm_gain).astype(jnp.bfloat16)
    return jnp.dot(normed, out_weight, preferred_element_type=jnp.float32).astype(jnp.bfloat16)
```

```python
import functools

import jax
import jax.numpy as jnp
import numpy as np
from jax import lax
from jax.experimental import pallas as pl
from jax.experimental.pallas import tpu as pltpu
from jax.sharding import PartitionSpec as P

DK = 128
SPAN = 64
LEVELS = 12
QUAD = 4
BLOCK = QUAD * SPAN
SCALE = [float(np.exp2(np.float32(-0.5 * l)) * np.float32(DK ** (-0.5))) for l in range(LEVELS)]
F32 = jnp.float32
BF16 = jnp.bfloat16


def bits_of(count):
    return count.bit_length() - 1


def block_states(quads):
    found = []
    for bit in range(bits_of(quads)):
        for first in range(0, quads, 2 << bit):
            found.append((bit, first))
    return found


def states_kernel(quads, group_bits, heads, k_ref, v_ref, st_ref, tot_ref, totb_ref, acc_ref):
    step = pl.program_id(0)

    @pl.when(step == 0)
    def _():
        acc_ref[...] = jnp.zeros_like(acc_ref)

    inner = block_states(quads)
    for h in range(heads):
        cols = slice(h * DK, (h + 1) * DK)
        level = []
        for u in range(quads):
            rows = slice(u * BLOCK, (u + 1) * BLOCK)
            level.append(
                lax.dot_general(
                    k_ref[rows, cols],
                    v_ref[rows, cols],
                    (((0,), (0,)), ((), ())),
                    preferred_element_type=F32,
                )
            )
        bit = 0
        while len(level) > 1:
            for pos in range(0, len(level), 2):
                slot = inner.index((bit, pos << bit))
                st_ref[0, slot, h] = level[pos].astype(BF16)
            level = [level[p] + level[p + 1] for p in range(0, len(level), 2)]
            bit += 1
        whole = level[0]
        for b in range(group_bits):
            st_ref[0, len(inner) + b, h] = acc_ref[b, h].astype(BF16)
        carry = whole
        for b in range(group_bits):
            low = (1 << b) - 1

            @pl.when(jnp.logical_and(step & low == low, step >> b & 1 == 0))
            def _(carry=carry, b=b):
                acc_ref[b, h] = carry

            carry = carry + acc_ref[b, h]

        @pl.when(step == pl.num_programs(0) - 1)
        def _(carry=carry):
            tot_ref[h] = carry
            totb_ref[h] = carry.astype(BF16)


def span_scalar(lam, lw_ref, h, level):
    return lw_ref[lam, h * LEVELS + level] * SCALE[level]


def scaled(q32, lams, lw_ref, h, level, on):
    parts = []
    for i in range(QUAD):
        s = span_scalar(lams[i], lw_ref, h, level)
        if on is not None:
            s = jnp.where(on, s, 0.0)
        parts.append((q32[i * SPAN : (i + 1) * SPAN] * s).astype(BF16))
    return jnp.concatenate(parts, axis=0)


def local_kernel(quads, group_bits, heads, j, lam_ref, lw_ref, q_ref, k_ref, v_ref, st_ref, out_ref):
    group = pl.program_id(0)
    inner = block_states(quads)
    base = (group * quads + j) * QUAD
    lams = [lam_ref[base + i] for i in range(QUAD)]
    row = lax.broadcasted_iota(jnp.int32, (SPAN, 2 * SPAN), 0)
    lane = lax.broadcasted_iota(jnp.int32, (SPAN, 2 * SPAN), 1)
    half = lane < SPAN
    low = lane <= row
    high = jnp.logical_and(lane >= SPAN, lane - SPAN <= row)
    level0 = bits_of(QUAD) + 1
    for h in range(heads):
        cols = slice(h * DK, (h + 1) * DK)
        q = q_ref[:, cols]
        v = v_ref[:, cols]
        scores = lax.dot_general(
            q, k_ref[:, cols], (((1,), (1,)), ((), ())), preferred_element_type=F32
        )
        rows = []
        for i in range(QUAD):
            c0 = span_scalar(lams[i], lw_ref, h, 0)
            c1 = span_scalar(lams[i], lw_ref, h, 1)
            c2 = span_scalar(lams[i], lw_ref, h, 2)
            left = scores[i * SPAN : (i + 1) * SPAN, : 2 * SPAN]
            right = scores[i * SPAN : (i + 1) * SPAN, 2 * SPAN :]
            diagonal = left if i < 2 else right
            if i % 2 == 0:
                diagonal = jnp.where(low, diagonal * c0, 0.0)
            else:
                diagonal = diagonal * jnp.where(half, c1, jnp.where(high, c0, 0.0))
            if i < 2:
                pair = (diagonal, jnp.zeros_like(diagonal))
            else:
                pair = (left * c2, diagonal)
            rows.append(jnp.concatenate([x.astype(BF16) for x in pair], axis=1))
        weights = jnp.concatenate(rows, axis=0)
        total = jnp.dot(weights, v, preferred_element_type=F32)
        q32 = q.astype(F32)
        left, right = [], []
        for b in range(bits_of(quads)):
            if j >> b & 1:
                slot = inner.index((b, (j >> b << b) - (1 << b)))
                left.append(scaled(q32, lams, lw_ref, h, level0 + b, None))
                right.append(st_ref[0, slot, h])
        for b in range(group_bits):
            level = level0 + bits_of(quads) + b
            left.append(scaled(q32, lams, lw_ref, h, level, group >> b & 1 == 1))
            right.append(st_ref[0, len(inner) + b, h])
        if left:
            total = total + jnp.dot(
                jnp.concatenate(left, axis=1),
                jnp.concatenate(right, axis=0),
                preferred_element_type=F32,
            )
        out_ref[0, :, cols] = total


def cross_kernel(quads, groups, ctx_bits, heads, j, pos_ref, lam_ref, lw_ref, loc_ref, q_ref, *rest):
    x_refs, out_ref = rest[:ctx_bits], rest[ctx_bits]
    group = pl.program_id(0)
    base = (group * quads + j) * QUAD
    lams = [lam_ref[base + i] for i in range(QUAD)]
    level0 = 1 + bits_of(QUAD) + bits_of(quads) + bits_of(groups)
    ctx = pos_ref[0]
    for h in range(heads):
        cols = slice(h * DK, (h + 1) * DK)
        q32 = q_ref[:, cols].astype(F32)
        total = loc_ref[0, :, cols]
        left = [
            scaled(q32, lams, lw_ref, h, level0 + b, ctx >> b & 1 == 1) for b in range(ctx_bits)
        ]
        right = [x_refs[b][h] for b in range(ctx_bits)]
        if left:
            total = total + jnp.dot(
                jnp.concatenate(left, axis=1),
                jnp.concatenate(right, axis=0),
                preferred_element_type=F32,
            )
        out_ref[0, :, cols] = total.astype(BF16)


def final_kernel(count, width, pos_ref, *refs):
    atts, gates, gains = refs[:count], refs[count : 2 * count], refs[2 * count : 3 * count]
    w_ref = refs[3 * count]
    out_ref, normed_ref, gated_ref = refs[-3:]

    @pl.when(pl.program_id(0) == 0)
    def _():
        square = None
        for k in range(count):
            gate = gates[k][...].astype(F32)
            att = atts[k][...].reshape(gate.shape).astype(F32)
            gated = att * (gate / (1.0 + jnp.exp(-gate)))
            gated_ref[k] = gated
            part = jnp.sum(gated * gated, axis=-1, keepdims=True)
            square = part if square is None else square + part
        inv = lax.rsqrt(square / (count * width) + 1e-6)
        me = pos_ref[1]
        for k in range(count):
            at = pl.multiple_of((me ^ k) * width, width)
            normed_ref[:, pl.ds(at, width)] = (gated_ref[k] * inv * gains[k][...]).astype(BF16)

    out_ref[...] = lax.dot_general(
        normed_ref[...], w_ref[...], (((1,), (1,)), ((), ())), preferred_element_type=F32
    ).astype(BF16)


def xor_swap(x, axis, bit):
    size = lax.axis_size(axis)
    return lax.ppermute(x, axis, [(i, i ^ bit) for i in range(size)])


def gather_weight(shard, ctx, head):
    c_size, h_size = lax.axis_size("ctx"), lax.axis_size("head")
    cols, depth = shard.shape[1], shard.shape[0]
    held = [(0, shard.T)]
    bit = h_size // 2
    while bit > 1:
        held = held + [(k ^ bit, xor_swap(p, "head", bit)) for k, p in held]
        bit //= 2
    inner = 2 if c_size % 2 == 0 else 1
    ring = c_size // inner
    steps = [held]
    for _ in range(ring - 1):
        perm = [(i, (i + inner) % c_size) for i in range(c_size)]
        steps.append([(k, lax.ppermute(p, "ctx", perm)) for k, p in steps[-1]])
    pieces = []
    for s, group in enumerate(steps):
        owner = (ctx - s * inner) % c_size
        for k, p in group:
            pieces.append((owner, k, p))
            if inner == 2:
                pieces.append((owner ^ 1, k, xor_swap(p, "ctx", 1)))
    full = []
    for owner, k, p in pieces:
        full.append((owner, k, p))
        if h_size > 1:
            full.append((owner, k ^ 1, xor_swap(p, "head", 1)))
    out = jnp.zeros((c_size * h_size * cols, depth), shard.dtype)
    for owner, k, p in full:
        at = (owner * h_size + (head ^ k)) * cols
        out = lax.dynamic_update_slice(out, p, (at, 0))
    return out


def smem():
    return pl.BlockSpec(memory_space=pltpu.SMEM)


def local(queries, keys, values, lam_index, level_weights, gate, norm_gain, out_weight):
    rows, width = queries.shape
    heads = level_weights.shape[1]
    c_size, h_size = lax.axis_size("ctx"), lax.axis_size("head")
    ctx, head = lax.axis_index("ctx"), lax.axis_index("head")
    own = rows // h_size
    groups = h_size
    quads = own // BLOCK
    group_bits, ctx_bits = bits_of(groups), bits_of(c_size)
    n_inner = len(block_states(quads))
    n_states = n_inner + group_bits
    model = gate.shape[1]
    pos = jnp.stack([ctx, head]).astype(jnp.int32)
    table = level_weights.reshape(level_weights.shape[0], heads * LEVELS)

    weight = gather_weight(out_weight, ctx, head)

    states, total, total_b = pl.pallas_call(
        functools.partial(states_kernel, quads, group_bits, heads),
        grid=(groups,),
        in_specs=[pl.BlockSpec((own, width), lambda s: (s, 0))] * 2,
        out_specs=[
            pl.BlockSpec((1, n_states, heads, DK, DK), lambda s: (s, 0, 0, 0, 0)),
            pl.BlockSpec((heads, DK, DK), lambda s: (0, 0, 0)),
            pl.BlockSpec((heads, DK, DK), lambda s: (0, 0, 0)),
        ],
        out_shape=[
            jax.ShapeDtypeStruct((groups, n_states, heads, DK, DK), BF16),
            jax.ShapeDtypeStruct((heads, DK, DK), F32),
            jax.ShapeDtypeStruct((heads, DK, DK), BF16),
        ],
        scratch_shapes=[pltpu.VMEM((max(group_bits, 1), heads, DK, DK), F32)],
        name="states",
        cost_estimate=pl.CostEstimate(
            flops=2 * rows * width * DK, bytes_accessed=4 * rows * width, transcendentals=0
        ),
    )(keys, values)

    cross = []
    running = total
    sending = total_b
    for b in range(ctx_bits):
        received = xor_swap(sending, "ctx", 1 << b)
        cross.append(received)
        if b + 1 < ctx_bits:
            running = running + received.astype(F32)
            sending = running.astype(BF16)

    row_block = lambda j: (lambda d: (d * quads + j, 0))
    locals_ = []
    for j in range(quads):
        locals_.append(
            pl.pallas_call(
                functools.partial(local_kernel, quads, group_bits, heads, j),
                grid=(groups,),
                in_specs=[smem(), smem()]
                + [pl.BlockSpec((BLOCK, width), row_block(j))] * 3
                + [pl.BlockSpec((1, n_states, heads, DK, DK), lambda d: (d, 0, 0, 0, 0))],
                out_specs=pl.BlockSpec((1, BLOCK, width), lambda d: (d, 0, 0)),
                out_shape=jax.ShapeDtypeStruct((groups, BLOCK, width), F32),
                name=f"local{j}",
                cost_estimate=pl.CostEstimate(
                    flops=2 * groups * BLOCK * width * 1024,
                    bytes_accessed=groups * BLOCK * width * 10,
                    transcendentals=0,
                ),
            )(lam_index, table, queries, keys, values, states)
        )

    out = None
    for j in range(quads):
        att = pl.pallas_call(
            functools.partial(cross_kernel, quads, groups, ctx_bits, heads, j),
            grid=(groups,),
            in_specs=[smem(), smem(), smem()]
            + [
                pl.BlockSpec((1, BLOCK, width), lambda d: (d, 0, 0)),
                pl.BlockSpec((BLOCK, width), row_block(j)),
            ]
            + [pl.BlockSpec((heads, DK, DK), lambda d: (0, 0, 0))] * ctx_bits,
            out_specs=pl.BlockSpec((1, BLOCK, width), lambda d: (d, 0, 0)),
            out_shape=jax.ShapeDtypeStruct((groups, BLOCK, width), BF16),
            name=f"cross{j}",
            cost_estimate=pl.CostEstimate(
                flops=2 * groups * BLOCK * width * DK * max(ctx_bits, 1),
                bytes_accessed=groups * BLOCK * width * 8,
                transcendentals=0,
            ),
        )(pos, lam_index, table, locals_[j], queries, *cross)
        received = []
        for k in range(1, h_size):
            piece = lax.dynamic_index_in_dim(att, head ^ k, 0, keepdims=False)
            received.append(xor_swap(piece, "head", k))
        grid_spec = pltpu.PrefetchScalarGridSpec(
            num_scalar_prefetch=1,
            grid=(model // 256,),
            in_specs=[pl.BlockSpec((1, BLOCK, width), lambda n, p: (p[1], 0, 0))]
            + [pl.BlockSpec((BLOCK, width), lambda n, p: (0, 0))] * (h_size - 1)
            + [
                pl.BlockSpec((BLOCK, width), functools.partial(lambda k, n, p: (j, p[1] ^ k), k))
                for k in range(h_size)
            ]
            + [
                pl.BlockSpec((1, width), functools.partial(lambda k, n, p: (0, p[1] ^ k), k))
                for k in range(h_size)
            ]
            + [pl.BlockSpec((256, model), lambda n, p: (n, 0))]
            + ([pl.BlockSpec(memory_space=pl.ANY)] if j else []),
            out_specs=pl.BlockSpec((BLOCK, 256), functools.partial(lambda j, n, p: (j, n), j)),
            scratch_shapes=[
                pltpu.VMEM((BLOCK, model), BF16),
                pltpu.VMEM((h_size, BLOCK, width), F32),
            ],
        )
        args = [pos, att, *received, *([gate] * h_size), *([norm_gain[None]] * h_size), weight]
        out = pl.pallas_call(
            functools.partial(final_kernel, h_size, width),
            grid_spec=grid_spec,
            out_shape=jax.ShapeDtypeStruct((own, model), BF16),
            input_output_aliases={len(args): 0} if j else {},
            name=f"final{j}",
            cost_estimate=pl.CostEstimate(
                flops=2 * BLOCK * model * model,
                bytes_accessed=2 * model * model + 6 * BLOCK * model,
                transcendentals=BLOCK * model,
            ),
        )(*args, *([out] if j else []))
    return out


def solution(mesh):
    in_specs = (
        P("ctx", "head"),
        P("ctx", "head"),
        P("ctx", "head"),
        P("ctx"),
        P(None, "head", None),
        P(("ctx", "head"), None),
        P(),
        P(None, ("ctx", "head")),
    )
    out_specs = P(("ctx", "head"), None)
    return jax.shard_map(local, mesh=mesh, in_specs=in_specs, out_specs=out_specs, check_vma=False)
```
